32 devices in a mesh: grp: 4 (over z), ch: 8 (over y, x, core).
Axes of the slice: x: 2, y: 2, z: 4, core: 2. Of those that a mesh axis runs over, the one named last changes fastest.
Arguments:
- features: bfloat16 [64, 64, 512], P(('grp', 'ch')), may hold values from -6 to 6
- live_counts: int32 [32], P(('grp', 'ch')), may hold values from 1 to 2, as said below
- neighbours: int32 [64, 27], P(('grp', 'ch')), may hold values from -1 to 63, as said below
- w_first: bfloat16 [27, 64, 64], replicated, may hold values from -0.21875 to 0.21875
- w_second: bfloat16 [27, 64, 64], replicated, may hold values from -0.21875 to 0.21875
- w_middle: bfloat16 [27, 128, 64], replicated, may hold values from -0.3125 to 0.3125
- w_coarse: bfloat16 [27, 256, 128], P(None, 'ch'), may hold values from -0.21875 to 0.21875
- w_project: bfloat16 [256, 64], P('ch'), may hold values from -0.75 to 0.75
- w_output: bfloat16 [64, 128], replicated, may hold values from -0.5 to 0.5
Outputs:
- mixed_out: bfloat16 [64, 64, 512], P(('grp', 'ch'))
The draws below stay inside these ranges and needn't reach their ends.
Inputs may be any that keep to these rules, and one draw needn't show every extreme that they name: Device d holds its live blocks in slots d * 2 to d * 2 + live_counts[d] - 1; the rest are padding. In every group of devices along ch one device holds exactly 2. `neighbours`: the live blocks occupy distinct positions of a lattice of 16 x 16 x (2 times the size of grp) positions; the devices with grp index g hold exactly the blocks of layers g * 2 to (g + 1) * 2 - 1 along z. Within a group, the device with ch index m (of n) holds blocks only in the tile of x from floor(2 m / n) * 8 to that plus 16 / 2 - 1 and y from (m mod (n / 2)) * 2 * 16 / n to that plus 2 * 16 / n - 1. For a live block b, entry 9 (dx + 1) + 3 (dy + 1) + dz + 1 is the block at b's position plus (dx, dy, dz), or -1 where that position is empty or off the lattice; entry 13 is b itself. Rows of padding slots are all -1, and no entry names a padding slot.
All inputs are finite; a program needn't handle non-finite values.
Results may differ from the reference program's by a relative error of at most 0.013.
Values may be sent and summed in bfloat16 or wider, within the bound.
A program may use at most 128 MiB of HBM per device.

```python
import jax
import jax.numpy as jnp
from jax import lax

C0 = 64
C1 = 128
C2 = 256
EDGE = 8
SIDE = 16
LAYERS = 2
BLK_DEV = 2
GROUP_BLOCKS = 16
BLOCKS = 64


def scene(key):
    base_key = jax.random.fold_in(key, 11)
    counts_key, choose_key, order_key = jax.random.split(base_key, 3)
    groups = BLOCKS // GROUP_BLOCKS
    members = GROUP_BLOCKS // BLK_DEV
    places = SIDE * SIDE * LAYERS
    tile_size = places // members
    half_members = members // 2
    tile_x = SIDE // 2
    tile_y = SIDE // half_members
    lowest = max(BLK_DEV // 2, 1)
    counts = jax.random.randint(counts_key, (groups, members), lowest, BLK_DEV + 1)
    fullest = jax.random.randint(choose_key, (groups, 1), 0, members)
    counts = jnp.where(jnp.arange(members)[None, :] == fullest, BLK_DEV, counts).astype(jnp.int32)
    member_keys = jax.random.split(order_key, groups * members)
    orders = jax.vmap(lambda one_key: jax.random.permutation(one_key, tile_size))(member_keys)
    local = orders.reshape(groups, members, tile_size)[:, :, :BLK_DEV].astype(jnp.int32)
    slot_index = jnp.arange(BLK_DEV, dtype=jnp.int32)[None, None, :]
    member_ids = jnp.arange(members, dtype=jnp.int32)[None, :, None]
    group_ids = jnp.arange(groups, dtype=jnp.int32)[:, None, None]
    living = slot_index < counts[:, :, None]
    coord_x = member_ids // half_members * tile_x + local // (tile_y * LAYERS)
    coord_y = member_ids % half_members * tile_y + local // LAYERS % tile_y
    coord_z = local % LAYERS + group_ids * LAYERS
    place_all = coord_z // LAYERS * places + coord_x * SIDE * LAYERS + coord_y * LAYERS + coord_z % LAYERS
    ids = group_ids * GROUP_BLOCKS + member_ids * BLK_DEV + slot_index
    target = jnp.where(living, place_all, groups * places).reshape(-1)
    block_id = jnp.full((groups * places,), -1, jnp.int32).at[target].set(ids.reshape(-1).astype(jnp.int32), mode='drop')
    columns = []
    for shift_x in (-1, 0, 1):
        for shift_y in (-1, 0, 1):
            for shift_z in (-1, 0, 1):
                next_x = coord_x + shift_x
                next_y = coord_y + shift_y
                next_z = coord_z + shift_z
                inside = (next_x >= 0) & (next_x < SIDE) & (next_y >= 0) & (next_y < SIDE) & (next_z >= 0) & (next_z < groups * LAYERS)
                place = next_z // LAYERS * places + next_x * SIDE * LAYERS + next_y * LAYERS + next_z % LAYERS
                found = jnp.take(block_id, jnp.clip(place, 0, groups * places - 1))
                columns.append(jnp.where(inside & living, found, -1))
    table = jnp.stack(columns, axis=-1).reshape(BLOCKS, 27).astype(jnp.int32)
    return (counts.reshape(-1), table)


def draw_live_counts(key, part):
    return scene(key)[0]


def draw_neighbours(key, part):
    return scene(key)[1]


def steps_of(own_key, shape, pieces, low, high):
    loudness = 1.0
    for axis_at, blocks in pieces:
        heights = jax.random.uniform(jax.random.fold_in(jax.random.fold_in(own_key, 6), axis_at), (blocks,), jnp.float32, low / len(pieces), high / len(pieces))
        loudness = loudness * jnp.repeat(jnp.exp(heights), shape[axis_at] // blocks).reshape((-1,) + (1,) * (len(shape) - 1 - axis_at))
    return loudness


def normal_values(stream_key, extent, width, reach, cuts=(), kind=jnp.bfloat16):
    level = steps_of(stream_key, extent, cuts, -0.22, 0.18) if cuts else 1.0
    values = jax.random.normal(stream_key, extent, jnp.float32) * width * level
    return jnp.minimum(jnp.maximum(values, -reach), reach).astype(kind)


def setup_inputs(seed: int = 0) -> dict:
    splits = jax.random.split(jax.random.key(seed), 10)
    features = normal_values(splits[0], (BLOCKS, C0, EDGE ** 3), 1.0, 6.0, ((0, 32),))
    live_counts = draw_live_counts(jax.random.fold_in(splits[9], 71), 0)
    neighbours = draw_neighbours(jax.random.fold_in(splits[9], 71), 0)
    w_first = normal_values(splits[3], (27, C0, C0), (27 * C0 // 2) ** -0.5, 0.21875)
    w_second = normal_values(splits[4], (27, C0, C0), (27 * C0 // 2) ** -0.5, 0.21875)
    w_middle = normal_values(splits[5], (27, C1, C0), (27 * C0 // 4) ** -0.5, 0.3125)
    w_coarse = normal_values(splits[6], (27, C2, C1), (27 * C1 // 4) ** -0.5, 0.21875, ((1, 8),))
    w_project = normal_values(splits[7], (C2, C0), (C2 // 4) ** -0.5, 0.75, ((0, 8),))
    w_output = normal_values(splits[8], (C0, 2 * C0), (2 * C0) ** -0.5, 0.5)
    return dict(features=features, live_counts=live_counts, neighbours=neighbours, w_first=w_first, w_second=w_second, w_middle=w_middle, w_coarse=w_coarse, w_project=w_project, w_output=w_output)


offsets = [(shift_x, shift_y, shift_z) for shift_x in (-1, 0, 1) for shift_y in (-1, 0, 1) for shift_z in (-1, 0, 1)]


def ranges_for(step_in, margin, length):
    if step_in < 0:
        return 0, margin, length - margin, length
    if step_in == 0:
        return margin, margin + length, 0, length
    return margin + length, length + 2 * margin, 0, margin


def extend(volume, neighbour_rows, margin):
    count_rows = neighbour_rows.shape[0]
    channels = volume.shape[1]
    length = volume.shape[2]
    side_out = length + 2 * margin
    result = jnp.zeros((count_rows, channels, side_out, side_out, side_out), jnp.float32)
    for column, (shift_x, shift_y, shift_z) in enumerate(offsets):
        target = neighbour_rows[:, column]
        safe_rows = jnp.clip(target, 0, volume.shape[0] - 1)
        low_x, high_x, from_x, till_x = ranges_for(shift_x, margin, length)
        low_y, high_y, from_y, till_y = ranges_for(shift_y, margin, length)
        low_z, high_z, from_z, till_z = ranges_for(shift_z, margin, length)
        portion = volume[safe_rows, :, from_x:till_x, from_y:till_y, from_z:till_z]
        portion = jnp.where((target >= 0)[:, None, None, None, None], portion, jnp.zeros_like(portion))
        result = result.at[:, :, low_x:high_x, low_y:high_y, low_z:high_z].set(portion)
    return result


def convolve(padded, weight):
    inside = padded.shape[2] - 2
    summed = None
    for column, (shift_x, shift_y, shift_z) in enumerate(offsets):
        window = padded[:, :, 1 + shift_x:1 + shift_x + inside, 1 + shift_y:1 + shift_y + inside, 1 + shift_z:1 + shift_z + inside]
        product_term = jnp.einsum("oc,bcxyz->boxyz", weight[column].astype(jnp.float32), window, precision=lax.Precision.HIGHEST)
        summed = product_term if summed is None else summed + product_term
    return summed


def layer(volume, neighbours, weight, batches):
    grouped = neighbours.reshape(batches, -1, 27)

    def one_batch(neighbour_rows):
        return jax.nn.gelu(convolve(extend(volume, neighbour_rows, 1), weight)).astype(jnp.bfloat16)

    output = lax.map(one_batch, grouped)
    return output.reshape((volume.shape[0],) + output.shape[2:])


def pooled(volume):
    count_rows, channels, length = volume.shape[0], volume.shape[1], volume.shape[2]
    halved = length // 2
    blocked = volume.astype(jnp.float32).reshape(count_rows, channels, halved, 2, halved, 2, halved, 2)
    return (jnp.sum(blocked, axis=(3, 5, 7)) * 0.125).astype(jnp.bfloat16)


def reference(features, live_counts, neighbours, w_first, w_second, w_middle, w_coarse, w_project, w_output):
    batches = BLOCKS // GROUP_BLOCKS
    volume = features.reshape(BLOCKS, C0, EDGE, EDGE, EDGE).astype(jnp.float32)
    first_out = layer(volume, neighbours, w_first, batches)
    second = layer(first_out.astype(jnp.float32), neighbours, w_second, batches)
    middle_in = pooled(second)
    middle = layer(middle_in.astype(jnp.float32), neighbours, w_middle, batches)
    coarse_in = pooled(middle)
    hidden = layer(coarse_in.astype(jnp.float32), neighbours, w_coarse, batches)
    coarse = jnp.einsum("ko,bkxyz->boxyz", w_project.astype(jnp.float32), hidden.astype(jnp.float32), precision=lax.Precision.HIGHEST).astype(jnp.bfloat16)
    factor = EDGE // coarse.shape[2]
    widened = jnp.repeat(jnp.repeat(jnp.repeat(coarse, factor, axis=2), factor, axis=3), factor, axis=4)
    skipped = jnp.einsum("oc,bcxyz->boxyz", w_output[:, :C0].astype(jnp.float32), second.astype(jnp.float32), precision=lax.Precision.HIGHEST)
    lifted = jnp.einsum("oc,bcxyz->boxyz", w_output[:, C0:].astype(jnp.float32), widened.astype(jnp.float32), precision=lax.Precision.HIGHEST)
    mixed_out = skipped + lifted
    slot_ids = jnp.arange(BLOCKS, dtype=jnp.int32)
    living = (slot_ids % BLK_DEV) < live_counts[slot_ids // BLK_DEV]
    mixed_out = jnp.where(living[:, None, None, None, None], mixed_out, jnp.zeros_like(mixed_out))
    return mixed_out.astype(jnp.bfloat16).reshape(BLOCKS, C0, EDGE ** 3)
```

```python
import functools

import jax
import jax.numpy as jnp
from jax import lax
from jax.experimental import pallas as pl
from jax.experimental.pallas import tpu as pltpu
from jax.sharding import PartitionSpec as P

MESH = pl.DeviceIdType.MESH
F32, BF16 = jnp.float32, jnp.bfloat16
STEPS = (-1, 0, 1)
OFFSETS = [(x, y, z) for x in STEPS for y in STEPS for z in STEPS]
PARTNERS = [(h, y, z) for h in (0, 1) for y in STEPS for z in STEPS if (h, y, z) != (0, 0, 0)]
PIECES = 3


def matmul_nt(left, right):
    return lax.dot_general(left, right, (((1,), (1,)), ((), ())), preferred_element_type=F32)


def rounded_gelu(value):
    return jax.nn.gelu(value).astype(BF16)


def kernel(grps, n, feat, live, neigh, w1_any, w2_any, wm_any, wc_any, wp_any, wo_any, out, levels, mats, sems):
    g, m = lax.axis_index("grp"), lax.axis_index("ch")
    q = n // 2
    half, tile = m // q, m % q
    slots, c0, voxels = feat.shape
    edge = round(voxels ** (1 / 3))
    c1 = wm_any.shape[1]

    def has(partner):
        _, y, z = partner
        return (tile + y >= 0) & (tile + y < q) & (g + z >= 0) & (g + z < grps)

    def coords(partner):
        h, y, z = partner
        return g + z, ((1 - half) if h else half) * q + tile + y

    barrier = pltpu.get_barrier_semaphore()
    for r in range(1, n):
        pl.semaphore_signal(barrier, inc=1, device_id=(g, (m + r) % n), device_id_type=MESH)
    far = [p for p in PARTNERS if p[2] != 0]
    for p in far:

        @pl.when(has(p))
        def _():
            pl.semaphore_signal(barrier, inc=1, device_id=coords(p), device_id_type=MESH)

    (w1, w2, wm, wo, wc, wp, b1, b2, bm, im_leaf, im_mid, im_coarse) = mats
    (local_sem, wsend, wrecv, psend, precv) = sems
    loads = [
        pltpu.make_async_copy(source, target, local_sem.at[i])
        for i, (source, target) in enumerate(
            [(w1_any, w1), (w2_any, w2), (wm_any, wm), (wo_any, wo), (wc_any, wc.at[m]), (wp_any, wp.at[m])]
        )
    ]
    for load in loads:
        load.start()

    def piece_of(level, partner):
        h, y, z = partner
        volume, caps = level["v"], level["caps"]
        length = volume.shape[0]
        pick_x = pl.ds((1 - half) * (length - 1), 1) if h else slice(None)
        pick_y = slice(None) if y == 0 else (pl.ds(length - 1, 1) if y > 0 else pl.ds(0, 1))
        if z == 0:
            return volume.at[pick_x, pick_y]
        return caps.at[1 if z > 0 else 0, pick_x, pick_y]

    def copy_to(level, index):
        h, y, z = PARTNERS[index]
        back = PARTNERS.index((h, -y, -z))
        return pltpu.make_async_remote_copy(
            src_ref=piece_of(level, PARTNERS[index]),
            dst_ref=level["got"][back],
            send_sem=level["send"].at[index],
            recv_sem=level["recv"].at[back],
            device_id=coords(PARTNERS[index]),
            device_id_type=MESH,
        )

    order = sorted(range(len(PARTNERS)), key=lambda i: -sum(abs(s) for s in PARTNERS[i]))

    def caps_of(level):
        volume, caps = level["v"], level["caps"]
        length = volume.shape[0]
        caps[0] = volume[:, :, 0:1, :]
        caps[1] = volume[:, :, length - 1 : length, :]

    def send(level):
        for i in order:

            @pl.when(has(PARTNERS[i]))
            def _():
                copy_to(level, i).start()

    def receive(level):
        for i in order:
            h, y, z = PARTNERS[i]

            @pl.when(has((h, -y, -z)))
            def _():
                copy_to(level, i).wait_recv()

    def extend(level):
        volume, ext, caps = level["v"], level["ext"], level["caps"]
        length, lanes = volume.shape[0], volume.shape[3]
        middle = lanes // 2
        lane = lax.broadcasted_iota(jnp.int32, (1, 1, 1, lanes), 3)
        upper = (lane >= middle).astype(jnp.int32)
        ext[1 : length + 1, 1 : length + 1, 1 : length + 1, :] = volume[...]
        firsts = {}
        for p in [(0, 0, 0)] + PARTNERS:
            a, b = coords(p)
            firsts[p] = jnp.where(has(p), (a * n + b) * 2, -8)

        def source_at(step):
            return slice(0, length) if step == 0 else (slice(0, 1) if step > 0 else slice(length - 1, length))

        def target_at(step):
            return slice(1, length + 1) if step == 0 else (slice(0, 1) if step < 0 else slice(length + 1, length + 2))

        for column, (x, y, z) in enumerate(OFFSETS):
            if (x, y, z) == (0, 0, 0):
                continue
            wanted = jnp.where(upper == 1, neigh[1, column], neigh[0, column])
            shape = tuple(length if s == 0 else 1 for s in (x, y, z)) + (lanes,)
            wanted = jnp.broadcast_to(wanted, shape)
            upper_full = jnp.broadcast_to(upper, shape)
            value = jnp.zeros(shape, F32)
            for h in (0, 1) if x else (0,):
                for cy in (0, y) if y else (0,):
                    for cz in (0, z) if z else (0,):
                        p = (h, cy, cz)
                        at_x = slice(0, 1) if h else source_at(x)
                        at_y = slice(0, 1) if cy else source_at(y)
                        at_z = slice(0, 1) if cz else source_at(z)
                        if p == (0, 0, 0):
                            if z:
                                found = caps[0 if z > 0 else 1, at_x, at_y, :, :]
                            else:
                                found = volume[at_x, at_y, at_z, :]
                        else:
                            found = level["got"][PARTNERS.index(p)][at_x, at_y, at_z, :]
                        swapped = jnp.concatenate([found[..., middle:], found[..., :middle]], axis=3)
                        value = jnp.where(
                            wanted == firsts[p] + upper_full,
                            found,
                            jnp.where(wanted == firsts[p] + 1 - upper_full, swapped, value),
                        )
            ext[target_at(x), target_at(y), target_at(z), :] = value

    taps = wc.shape[1]

    def weight_copy(part, r):
        first, last = taps * part // PIECES, taps * (part + 1) // PIECES
        return pltpu.make_async_remote_copy(
            src_ref=wc.at[m, pl.ds(first, last - first)],
            dst_ref=wc.at[m, pl.ds(first, last - first)],
            send_sem=wsend.at[part, r - 1],
            recv_sem=wrecv.at[part, r - 1],
            device_id=(g, (m + r) % n),
            device_id_type=MESH,
        )

    def weight_arrival(part, r):
        first, last = taps * part // PIECES, taps * (part + 1) // PIECES
        other = (m + n - r) % n
        return pltpu.make_async_remote_copy(
            src_ref=wc.at[other, pl.ds(first, last - first)],
            dst_ref=wc.at[other, pl.ds(first, last - first)],
            send_sem=wsend.at[part, r - 1],
            recv_sem=wrecv.at[part, r - 1],
            device_id=(g, other),
            device_id_type=MESH,
        )

    def project_copy(r, other):
        return pltpu.make_async_remote_copy(
            src_ref=wp.at[other],
            dst_ref=wp.at[other],
            send_sem=psend.at[r - 1],
            recv_sem=precv.at[r - 1],
            device_id=(g, (m + r) % n),
            device_id_type=MESH,
        )

    def send_weights(part):
        for r in range(1, n):
            weight_copy(part, r).start()

    def diagonal(matrix):
        empty = jnp.zeros_like(matrix)
        return jnp.concatenate([matrix, empty], axis=1), jnp.concatenate([empty, matrix], axis=1)

    def fill_diagonal(weights, target):
        rows, width = weights.shape[1], 2 * weights.shape[2]
        for t in range(weights.shape[0]):
            top, bottom = diagonal(weights[t])
            at = (t % 9) * width
            target[t // 9, 0:rows, at : at + width] = top
            target[t // 9, rows : 2 * rows, at : at + width] = bottom

    def convolve_leaf(level, weights):
        ext, length, lanes = level["ext"], edge, level["v"].shape[3]
        for k in range(9):
            y, z = k // 3, k % 3
            rows = ext[:, y : y + length, z : z + length, :].reshape(length + 2, length * length, lanes)
            im_leaf[:, :, k * lanes : (k + 1) * lanes] = rows.astype(BF16)
        total = None
        for x in range(3):
            window = im_leaf[x : x + length].reshape(length**3, 9 * lanes)
            term = matmul_nt(window, weights[x])
            total = term if total is None else total + term
        return rounded_gelu(total)

    leaf_a, leaf_b, mid, low = levels
    packed = feat[...].reshape(slots * c0, voxels).astype(F32)
    leaf_a["v"][...] = packed.T.reshape(edge, edge, edge, slots * c0)
    caps_of(leaf_a)
    peers = n - 1
    for p in far:
        peers = peers + has(p).astype(jnp.int32)
    pl.semaphore_wait(barrier, peers)

    send(leaf_a)
    loads[0].wait()
    fill_diagonal(w1, b1)
    loads[4].wait()
    loads[5].wait()
    send_weights(0)
    for r in range(1, n):
        project_copy(r, m).start()
    receive(leaf_a)
    extend(leaf_a)
    first = convolve_leaf(leaf_a, b1)

    leaf_b["v"][...] = first.astype(F32).reshape(edge, edge, edge, slots * c0)
    caps_of(leaf_b)
    send(leaf_b)
    send_weights(1)
    loads[1].wait()
    fill_diagonal(w2, b2)
    receive(leaf_b)
    extend(leaf_b)
    second = convolve_leaf(leaf_b, b2)

    def halving(length):
        small = length // 2
        row = lax.broadcasted_iota(jnp.int32, (small**3, length**3), 0)
        column = lax.broadcasted_iota(jnp.int32, (small**3, length**3), 1)
        x, y, z = column // (length * length), column // length % length, column % length
        hit = row == (x // 2) * small * small + (y // 2) * small + z // 2
        return jnp.where(hit, 0.125, 0.0).astype(BF16)

    side = edge // 2
    pooled = jnp.dot(halving(edge), second, preferred_element_type=F32).astype(BF16).astype(F32)
    for x in range(side):
        for y in range(side):
            at = (x * side + y) * side
            mid["v"][x, y] = pooled[at : at + side]
    caps_of(mid)
    send(mid)
    send_weights(2)
    loads[2].wait()
    fill_diagonal(wm, bm)
    receive(mid)
    extend(mid)
    lanes = slots * c0
    for k in range(9):
        ty, tz = k // 3, k % 3
        for y in range(side):
            im_mid[:, y * side : (y + 1) * side, k * lanes : (k + 1) * lanes] = mid["ext"][:, y + ty, tz : tz + side, :]
    total = None
    for x in range(3):
        window = im_mid[x : x + side].astype(BF16).reshape(side**3, 9 * lanes)
        term = matmul_nt(window, bm[x])
        total = term if total is None else total + term
    middle = rounded_gelu(total)

    small = side // 2
    pooled = jnp.dot(halving(side), middle, preferred_element_type=F32).astype(BF16).astype(F32)
    for x in range(small):
        for y in range(small):
            at = (x * small + y) * small
            low["v"][x, y] = pooled[at : at + small]
    caps_of(low)
    send(low)
    loads[3].wait()
    skip_top, skip_bottom = diagonal(wo[:, :c0])
    lift_top, lift_bottom = diagonal(wo[:, c0:])
    skip_weights = jnp.concatenate([skip_top, skip_bottom], axis=0)
    lift_weights = jnp.concatenate([lift_top, lift_bottom], axis=0)
    mixed = matmul_nt(skip_weights, second)
    for part in range(PIECES):
        for r in range(1, n):
            weight_arrival(part, r).wait_recv()
    for r in range(1, n):
        project_copy(r, (m + n - r) % n).wait_recv()
    receive(low)
    extend(low)
    cells = small**3
    for t in range(taps):
        tx, ty, tz = t // 9, t // 3 % 3, t % 3
        for b in range(slots):
            for x in range(small):
                for y in range(small):
                    at = b * cells + (x * small + y) * small
                    im_coarse[at : at + small, t * c1 : (t + 1) * c1] = low["ext"][
                        x + tx, y + ty, tz : tz + small, b * c1 : (b + 1) * c1
                    ]
    total = None
    c2 = n * wc.shape[2]
    for t in range(taps):
        term = matmul_nt(im_coarse[:, t * c1 : (t + 1) * c1].astype(BF16), wc[:, t].reshape(c2, c1))
        total = term if total is None else total + term
    hidden = rounded_gelu(total)
    coarse = jnp.dot(hidden, wp[...].reshape(c2, c0), preferred_element_type=F32)
    coarse = jnp.concatenate([coarse[b * cells : (b + 1) * cells] for b in range(slots)], axis=1).astype(BF16)
    row = lax.broadcasted_iota(jnp.int32, (voxels, cells), 0)
    column = lax.broadcasted_iota(jnp.int32, (voxels, cells), 1)
    factor = edge // small
    x, y, z = row // (edge * edge), row // edge % edge, row % edge
    spread = column == (x // factor) * small * small + (y // factor) * small + z // factor
    spread = jnp.where(spread, 1.0, 0.0).astype(BF16)
    widened = jnp.dot(spread, coarse, preferred_element_type=F32).astype(BF16)
    mixed = mixed + matmul_nt(lift_weights, widened)
    owner = lax.broadcasted_iota(jnp.int32, mixed.shape, 0) // c0
    mixed = jnp.where(owner < live[0], mixed, 0.0).astype(BF16)
    for b in range(slots):
        out[b] = mixed[b * c0 : (b + 1) * c0]

    for level in levels:
        for i in order:

            @pl.when(has(PARTNERS[i]))
            def _():
                copy_to(level, i).wait_send()

    for r in range(1, n):
        for part in range(PIECES):
            weight_copy(part, r).wait_send()
        project_copy(r, m).wait_send()


def level_scratch(length, lanes):
    def got(partner):
        h, y, z = partner
        return pltpu.VMEM((1 if h else length, 1 if y else length, 1 if z else length, lanes), F32)

    return dict(
        v=pltpu.VMEM((length, length, length, lanes), F32),
        caps=pltpu.VMEM((2, length, length, 1, lanes), F32),
        ext=pltpu.VMEM((length + 2,) * 3 + (lanes,), F32),
        got=[got(p) for p in PARTNERS],
        send=pltpu.SemaphoreType.DMA((len(PARTNERS),)),
        recv=pltpu.SemaphoreType.DMA((len(PARTNERS),)),
    )


def shards(grps, n, features, live_counts, neighbours, w_first, w_second, w_middle, w_coarse, w_project, w_output):
    slots, c0, voxels = features.shape
    edge = round(voxels ** (1 / 3))
    taps, c1 = w_middle.shape[:2]
    lanes = slots * c0
    side, small = edge // 2, edge // 4
    levels = [
        level_scratch(edge, lanes),
        level_scratch(edge, lanes),
        level_scratch(side, lanes),
        level_scratch(small, slots * c1),
    ]
    mats = [
        pltpu.VMEM(w_first.shape, BF16),
        pltpu.VMEM(w_second.shape, BF16),
        pltpu.VMEM(w_middle.shape, BF16),
        pltpu.VMEM(w_output.shape, BF16),
        pltpu.VMEM((n,) + w_coarse.shape, BF16),
        pltpu.VMEM((n,) + w_project.shape, BF16),
        pltpu.VMEM((3, lanes, 9 * lanes), BF16),
        pltpu.VMEM((3, lanes, 9 * lanes), BF16),
        pltpu.VMEM((3, slots * c1, 9 * lanes), BF16),
        pltpu.VMEM((edge + 2, edge * edge, 9 * lanes), BF16),
        pltpu.VMEM((side + 2, side * side, 9 * lanes), F32),
        pltpu.VMEM((slots * small**3, taps * c1), F32),
    ]
    sems = [
        pltpu.SemaphoreType.DMA((6,)),
        pltpu.SemaphoreType.DMA((PIECES, n - 1)),
        pltpu.SemaphoreType.DMA((PIECES, n - 1)),
        pltpu.SemaphoreType.DMA((n - 1,)),
        pltpu.SemaphoreType.DMA((n - 1,)),
    ]
    smem = pl.BlockSpec(memory_space=pltpu.SMEM)
    vmem = pl.BlockSpec(memory_space=pltpu.VMEM)
    stay = pl.BlockSpec(memory_space=pl.ANY)
    return pl.pallas_call(
        functools.partial(kernel, grps, n),
        out_shape=jax.ShapeDtypeStruct(features.shape, BF16),
        in_specs=[vmem, smem, smem] + [stay] * 6,
        out_specs=vmem,
        scratch_shapes=[levels, mats, sems],
        compiler_params=pltpu.CompilerParams(collective_id=0, has_side_effects=True),
    )(features, live_counts, neighbours, w_first, w_second, w_middle, w_coarse, w_project, w_output)


def solution(mesh):
    in_specs = (
        P(("grp", "ch"), None, None),
        P(("grp", "ch")),
        P(("grp", "ch"), None),
        P(),
        P(),
        P(),
        P(None, "ch", None),
        P("ch", None),
        P(),
    )
    return jax.shard_map(
        functools.partial(shards, mesh.shape["grp"], mesh.shape["ch"]),
        mesh=mesh,
        in_specs=in_specs,
        out_specs=P(("grp", "ch"), None, None),
        check_vma=False,
    )
```

```python
import functools

import jax
import jax.numpy as jnp
from jax import lax
from jax.experimental import pallas as pl
from jax.experimental.pallas import tpu as pltpu
from jax.sharding import PartitionSpec as P

MESH = pl.DeviceIdType.MESH
F32, BF16 = jnp.float32, jnp.bfloat16
STEPS = (-1, 0, 1)
OFFSETS = [(x, y, z) for x in STEPS for y in STEPS for z in STEPS]
PARTNERS = [(h, y, z) for h in (0, 1) for y in STEPS for z in STEPS if (h, y, z) != (0, 0, 0)]
PIECES = 3


def matmul_nt(left, right):
    return lax.dot_general(left, right, (((1,), (1,)), ((), ())), preferred_element_type=F32)


def rounded_gelu(value):
    return jax.nn.gelu(value).astype(BF16)


def kernel(grps, n, feat, live, neigh, w1_any, w2_any, wm_any, wc_any, wp_any, wo_any, out, levels, mats, sems):
    g, m = lax.axis_index("grp"), lax.axis_index("ch")
    q = n // 2
    half, tile = m // q, m % q
    slots, c0, voxels = feat.shape
    edge = round(voxels ** (1 / 3))
    c1 = wm_any.shape[2]

    def has(partner):
        _, y, z = partner
        return (tile + y >= 0) & (tile + y < q) & (g + z >= 0) & (g + z < grps)

    def coords(partner):
        h, y, z = partner
        return g + z, ((1 - half) if h else half) * q + tile + y

    barrier = pltpu.get_barrier_semaphore()
    for r in range(1, n):
        pl.semaphore_signal(barrier, inc=1, device_id=(g, (m + r) % n), device_id_type=MESH)
    far = [p for p in PARTNERS if p[2] != 0]
    for p in far:

        @pl.when(has(p))
        def _():
            pl.semaphore_signal(barrier, inc=1, device_id=coords(p), device_id_type=MESH)

    (w1, w2, wm, wo, wc, wp, b1, b2, bm, im_leaf, im_mid, im_coarse) = mats
    (local_sem, wsend, wrecv, psend, precv) = sems
    loads = [
        pltpu.make_async_copy(source, target, local_sem.at[i])
        for i, (source, target) in enumerate(
            [(w1_any, w1), (w2_any, w2), (wm_any, wm), (wo_any, wo), (wc_any, wc.at[m]), (wp_any, wp.at[m])]
        )
    ]
    for load in loads:
        load.start()

    def piece_of(level, partner):
        h, y, z = partner
        volume, caps = level["v"], level["caps"]
        length = volume.shape[0]
        pick_x = pl.ds((1 - half) * (length - 1), 1) if h else slice(None)
        pick_y = slice(None) if y == 0 else (pl.ds(length - 1, 1) if y > 0 else pl.ds(0, 1))
        if z == 0:
            return volume.at[pick_x, pick_y]
        return caps.at[1 if z > 0 else 0, pick_x, pick_y]

    def copy_to(level, index):
        h, y, z = PARTNERS[index]
        back = PARTNERS.index((h, -y, -z))
        return pltpu.make_async_remote_copy(
            src_ref=piece_of(level, PARTNERS[index]),
            dst_ref=level["got"][back],
            send_sem=level["send"].at[index],
            recv_sem=level["recv"].at[back],
            device_id=coords(PARTNERS[index]),
            device_id_type=MESH,
        )

    order = sorted(range(len(PARTNERS)), key=lambda i: -sum(abs(s) for s in PARTNERS[i]))

    def caps_of(level):
        volume, caps = level["v"], level["caps"]
        length = volume.shape[0]
        caps[0] = volume[:, :, 0:1, :]
        caps[1] = volume[:, :, length - 1 : length, :]

    def send(level):
        for i in order:

            @pl.when(has(PARTNERS[i]))
            def _():
                copy_to(level, i).start()

    def receive(level):
        for i in order:
            h, y, z = PARTNERS[i]

            @pl.when(has((h, -y, -z)))
            def _():
                copy_to(level, i).wait_recv()

    def extend(level):
        volume, ext, caps = level["v"], level["ext"], level["caps"]
        length, lanes = volume.shape[0], volume.shape[3]
        middle = lanes // 2
        lane = lax.broadcasted_iota(jnp.int32, (1, 1, 1, lanes), 3)
        upper = (lane >= middle).astype(jnp.int32)
        ext[1 : length + 1, 1 : length + 1, 1 : length + 1, :] = volume[...]
        firsts = {}
        for p in [(0, 0, 0)] + PARTNERS:
            a, b = coords(p)
            firsts[p] = jnp.where(has(p), (a * n + b) * 2, -8)

        def source_at(step):
            return slice(0, length) if step == 0 else (slice(0, 1) if step > 0 else slice(length - 1, length))

        def target_at(step):
            return slice(1, length + 1) if step == 0 else (slice(0, 1) if step < 0 else slice(length + 1, length + 2))

        for column, (x, y, z) in enumerate(OFFSETS):
            if (x, y, z) == (0, 0, 0):
                continue
            wanted = jnp.where(upper == 1, neigh[1, column], neigh[0, column])
            shape = tuple(length if s == 0 else 1 for s in (x, y, z)) + (lanes,)
            wanted = jnp.broadcast_to(wanted, shape)
            upper_full = jnp.broadcast_to(upper, shape)
            value = jnp.zeros(shape, F32)
            for h in (0, 1) if x else (0,):
                for cy in (0, y) if y else (0,):
                    for cz in (0, z) if z else (0,):
                        p = (h, cy, cz)
                        at_x = slice(0, 1) if h else source_at(x)
                        at_y = slice(0, 1) if cy else source_at(y)
                        at_z = slice(0, 1) if cz else source_at(z)
                        if p == (0, 0, 0):
                            if z:
                                found = caps[0 if z > 0 else 1, at_x, at_y, :, :]
                            else:
                                found = volume[at_x, at_y, at_z, :]
                        else:
                            found = level["got"][PARTNERS.index(p)][at_x, at_y, at_z, :]
                        swapped = jnp.concatenate([found[..., middle:], found[..., :middle]], axis=3)
                        value = jnp.where(
                            wanted == firsts[p] + upper_full,
                            found,
                            jnp.where(wanted == firsts[p] + 1 - upper_full, swapped, value),
                        )
            ext[target_at(x), target_at(y), target_at(z), :] = value

    taps = wc.shape[1]

    pairs = n // 2
    pair, core = m // 2, m % 2
    partner = pair * 2 + 1 - core

    def weight_copies(part, role, r):
        first, last = taps * part // PIECES, taps * (part + 1) // PIECES
        other = (pair + pairs - r) % pairs * 2
        owner, came = [(m, partner), (m, other + core), (other + core, other + 1 - core)][role]
        target = (pair + r) % pairs * 2 + core if role == 1 else partner
        lane = (0, r, pairs - 1 + r)[role]

        def copy(who):
            spot = wc.at[who, pl.ds(first, last - first)]
            return pltpu.make_async_remote_copy(
                src_ref=spot,
                dst_ref=spot,
                send_sem=wsend.at[part, lane],
                recv_sem=wrecv.at[part, lane],
                device_id=(g, target),
                device_id_type=MESH,
            )

        return functools.partial(copy, owner), functools.partial(copy, came)

    def project_copy(r, other):
        return pltpu.make_async_remote_copy(
            src_ref=wp.at[other],
            dst_ref=wp.at[other],
            send_sem=psend.at[r - 1],
            recv_sem=precv.at[r - 1],
            device_id=(g, (m + r) % n),
            device_id_type=MESH,
        )

    def send_weights(part):
        for r in range(1, pairs):
            weight_copies(part, 1, r)[0]().start()
        weight_copies(part, 0, 0)[0]().start()

    def hand_on(part):
        for r in range(1, pairs):
            weight_copies(part, 1, r)[1]().wait_recv()
            weight_copies(part, 2, r)[0]().start()

    def diagonal(matrix):
        empty = jnp.zeros_like(matrix)
        return jnp.concatenate([matrix, empty], axis=1), jnp.concatenate([empty, matrix], axis=1)

    def fill_diagonal(weights, target):
        rows, width = weights.shape[1], 2 * weights.shape[2]
        for t in range(weights.shape[0]):
            top, bottom = diagonal(weights[t])
            at = (t % 9) * width
            target[t // 9, 0:rows, at : at + width] = top
            target[t // 9, rows : 2 * rows, at : at + width] = bottom

    def fill_upright(weights, target):
        rows, width = weights.shape[1:]
        for t in range(weights.shape[0]):
            empty = jnp.zeros((rows, width), BF16)
            for b in range(slots):
                at = (t % 9 * slots + b) * rows
                for other in range(slots):
                    there = weights[t] if other == b else empty
                    target[t // 9, at : at + rows, other * width : (other + 1) * width] = there

    def convolve_leaf(level, weights):
        ext, length, lanes = level["ext"], edge, level["v"].shape[3]
        for k in range(9):
            y, z = k // 3, k % 3
            rows = ext[:, y : y + length, z : z + length, :].reshape(length + 2, length * length, lanes)
            im_leaf[:, :, k * lanes : (k + 1) * lanes] = rows.astype(BF16)
        total = None
        for x in range(3):
            window = im_leaf[x : x + length].reshape(length**3, 9 * lanes)
            term = matmul_nt(window, weights[x])
            total = term if total is None else total + term
        return rounded_gelu(total)

    leaf_a, leaf_b, mid, low = levels
    packed = feat[...].reshape(slots * c0, voxels).astype(F32)
    leaf_a["v"][...] = packed.T.reshape(edge, edge, edge, slots * c0)
    caps_of(leaf_a)
    peers = n - 1
    for p in far:
        peers = peers + has(p).astype(jnp.int32)
    pl.semaphore_wait(barrier, peers)

    send(leaf_a)
    loads[0].wait()
    fill_diagonal(w1, b1)
    loads[4].wait()
    loads[5].wait()
    send_weights(0)
    for r in range(1, n):
        project_copy(r, m).start()
    receive(leaf_a)
    send_weights(1)
    extend(leaf_a)
    first = convolve_leaf(leaf_a, b1)

    leaf_b["v"][...] = first.astype(F32).reshape(edge, edge, edge, slots * c0)
    caps_of(leaf_b)
    send(leaf_b)
    loads[1].wait()
    fill_diagonal(w2, b2)
    hand_on(0)
    receive(leaf_b)
    send_weights(2)
    extend(leaf_b)
    second = convolve_leaf(leaf_b, b2)

    def halving(length):
        small = length // 2
        row = lax.broadcasted_iota(jnp.int32, (small**3, length**3), 0)
        column = lax.broadcasted_iota(jnp.int32, (small**3, length**3), 1)
        x, y, z = column // (length * length), column // length % length, column % length
        hit = row == (x // 2) * small * small + (y // 2) * small + z // 2
        return jnp.where(hit, 0.125, 0.0).astype(BF16)

    side = edge // 2
    pooled = jnp.dot(halving(edge), second, preferred_element_type=F32).astype(BF16).astype(F32)
    for x in range(side):
        for y in range(side):
            at = (x * side + y) * side
            mid["v"][x, y] = pooled[at : at + side]
    caps_of(mid)
    send(mid)
    loads[2].wait()
    fill_upright(wm, bm)
    hand_on(1)
    receive(mid)
    extend(mid)
    lanes = slots * c0
    for k in range(9):
        ty, tz = k // 3, k % 3
        for y in range(side):
            im_mid[:, y * side : (y + 1) * side, k * lanes : (k + 1) * lanes] = mid["ext"][:, y + ty, tz : tz + side, :]
    total = None
    for x in range(3):
        window = im_mid[x : x + side].astype(BF16).reshape(side**3, 9 * lanes)
        term = jnp.dot(window, bm[x], preferred_element_type=F32)
        total = term if total is None else total + term
    middle = rounded_gelu(total)

    small = side // 2
    pooled = jnp.dot(halving(side), middle, preferred_element_type=F32).astype(BF16).astype(F32)
    for x in range(small):
        for y in range(small):
            at = (x * small + y) * small
            low["v"][x, y] = pooled[at : at + small]
    caps_of(low)
    send(low)
    loads[3].wait()
    skip_top, skip_bottom = diagonal(wo[:, :c0])
    lift_top, lift_bottom = diagonal(wo[:, c0:])
    skip_weights = jnp.concatenate([skip_top, skip_bottom], axis=0)
    lift_weights = jnp.concatenate([lift_top, lift_bottom], axis=0)
    mixed = matmul_nt(skip_weights, second)
    hand_on(2)
    for part in range(PIECES):
        weight_copies(part, 0, 0)[1]().wait_recv()
        for r in range(1, pairs):
            weight_copies(part, 2, r)[1]().wait_recv()
    for r in range(1, n):
        project_copy(r, (m + n - r) % n).wait_recv()
    receive(low)
    extend(low)
    cells = small**3
    for t in range(taps):
        tx, ty, tz = t // 9, t // 3 % 3, t % 3
        for b in range(slots):
            for x in range(small):
                for y in range(small):
                    at = b * cells + (x * small + y) * small
                    im_coarse[at : at + small, t * c1 : (t + 1) * c1] = low["ext"][
                        x + tx, y + ty, tz : tz + small, b * c1 : (b + 1) * c1
                    ]
    total = None
    c2 = n * wc.shape[2]
    for t in range(taps):
        term = matmul_nt(im_coarse[:, t * c1 : (t + 1) * c1].astype(BF16), wc[:, t].reshape(c2, c1))
        total = term if total is None else total + term
    hidden = rounded_gelu(total)
    coarse = jnp.dot(hidden, wp[...].reshape(c2, c0), preferred_element_type=F32)
    coarse = jnp.concatenate([coarse[b * cells : (b + 1) * cells] for b in range(slots)], axis=1).astype(BF16)
    row = lax.broadcasted_iota(jnp.int32, (voxels, cells), 0)
    column = lax.broadcasted_iota(jnp.int32, (voxels, cells), 1)
    factor = edge // small
    x, y, z = row // (edge * edge), row // edge % edge, row % edge
    spread = column == (x // factor) * small * small + (y // factor) * small + z // factor
    spread = jnp.where(spread, 1.0, 0.0).astype(BF16)
    widened = jnp.dot(spread, coarse, preferred_element_type=F32).astype(BF16)
    mixed = mixed + matmul_nt(lift_weights, widened)
    owner = lax.broadcasted_iota(jnp.int32, mixed.shape, 0) // c0
    mixed = jnp.where(owner < live[0], mixed, 0.0).astype(BF16)
    for b in range(slots):
        out[b] = mixed[b * c0 : (b + 1) * c0]

    for level in levels:
        for i in order:

            @pl.when(has(PARTNERS[i]))
            def _():
                copy_to(level, i).wait_send()

    for r in range(1, n):
        project_copy(r, m).wait_send()
    for part in range(PIECES):
        weight_copies(part, 0, 0)[0]().wait_send()
        for r in range(1, pairs):
            weight_copies(part, 1, r)[0]().wait_send()
            weight_copies(part, 2, r)[0]().wait_send()


def level_scratch(length, lanes):
    def got(partner):
        h, y, z = partner
        return pltpu.VMEM((1 if h else length, 1 if y else length, 1 if z else length, lanes), F32)

    return dict(
        v=pltpu.VMEM((length, length, length, lanes), F32),
        caps=pltpu.VMEM((2, length, length, 1, lanes), F32),
        ext=pltpu.VMEM((length + 2,) * 3 + (lanes,), F32),
        got=[got(p) for p in PARTNERS],
        send=pltpu.SemaphoreType.DMA((len(PARTNERS),)),
        recv=pltpu.SemaphoreType.DMA((len(PARTNERS),)),
    )


def shards(grps, n, features, live_counts, neighbours, w_first, w_second, w_middle, w_coarse, w_project, w_output):
    slots, c0, voxels = features.shape
    edge = round(voxels ** (1 / 3))
    w_middle = jnp.swapaxes(w_middle, 1, 2)
    taps, _, c1 = w_middle.shape
    lanes = slots * c0
    side, small = edge // 2, edge // 4
    levels = [
        level_scratch(edge, lanes),
        level_scratch(edge, lanes),
        level_scratch(side, lanes),
        level_scratch(small, slots * c1),
    ]
    mats = [
        pltpu.VMEM(w_first.shape, BF16),
        pltpu.VMEM(w_second.shape, BF16),
        pltpu.VMEM(w_middle.shape, BF16),
        pltpu.VMEM(w_output.shape, BF16),
        pltpu.VMEM((n,) + w_coarse.shape, BF16),
        pltpu.VMEM((n,) + w_project.shape, BF16),
        pltpu.VMEM((3, lanes, 9 * lanes), BF16),
        pltpu.VMEM((3, lanes, 9 * lanes), BF16),
        pltpu.VMEM((3, 9 * lanes, slots * c1), BF16),
        pltpu.VMEM((edge + 2, edge * edge, 9 * lanes), BF16),
        pltpu.VMEM((side + 2, side * side, 9 * lanes), F32),
        pltpu.VMEM((slots * small**3, taps * c1), F32),
    ]
    sems = [
        pltpu.SemaphoreType.DMA((6,)),
        pltpu.SemaphoreType.DMA((PIECES, n - 1)),
        pltpu.SemaphoreType.DMA((PIECES, n - 1)),
        pltpu.SemaphoreType.DMA((n - 1,)),
        pltpu.SemaphoreType.DMA((n - 1,)),
    ]
    smem = pl.BlockSpec(memory_space=pltpu.SMEM)
    vmem = pl.BlockSpec(memory_space=pltpu.VMEM)
    stay = pl.BlockSpec(memory_space=pl.ANY)
    return pl.pallas_call(
        functools.partial(kernel, grps, n),
        out_shape=jax.ShapeDtypeStruct(features.shape, BF16),
        in_specs=[vmem, smem, smem] + [stay] * 6,
        out_specs=vmem,
        scratch_shapes=[levels, mats, sems],
        compiler_params=pltpu.CompilerParams(collective_id=0, has_side_effects=True),
    )(features, live_counts, neighbours, w_first, w_second, w_middle, w_coarse, w_project, w_output)


def solution(mesh):
    in_specs = (
        P(("grp", "ch"), None, None),
        P(("grp", "ch")),
        P(("grp", "ch"), None),
        P(),
        P(),
        P(),
        P(None, "ch", None),
        P("ch", None),
        P(),
    )
    return jax.shard_map(
        functools.partial(shards, mesh.shape["grp"], mesh.shape["ch"]),
        mesh=mesh,
        in_specs=in_specs,
        out_specs=P(("grp", "ch"), None, None),
        check_vma=False,
    )
```

```python
import functools

import jax
import jax.numpy as jnp
from jax import lax
from jax.experimental import pallas as pl
from jax.experimental.pallas import tpu as pltpu
from jax.sharding import PartitionSpec as P

MESH = pl.DeviceIdType.MESH
F32, BF16 = jnp.float32, jnp.bfloat16
STEPS = (-1, 0, 1)
OFFSETS = [(x, y, z) for x in STEPS for y in STEPS for z in STEPS]
PARTNERS = [(h, y, z) for h in (0, 1) for y in STEPS for z in STEPS if (h, y, z) != (0, 0, 0)]
PIECES = 3


def matmul_nt(left, right):
    return lax.dot_general(left, right, (((1,), (1,)), ((), ())), preferred_element_type=F32)


def rounded_gelu(value):
    return jax.nn.gelu(value).astype(BF16)


def kernel(grps, n, feat_any, live, neigh, w1_any, w2_any, wm_any, wc_any, wp_any, wo_any, out, levels, mats, sems):
    g, m = lax.axis_index("grp"), lax.axis_index("ch")
    q = n // 2
    half, tile = m // q, m % q
    slots, c0, voxels = feat_any.shape
    edge = round(voxels ** (1 / 3))
    c1 = wm_any.shape[2]

    def has(partner):
        _, y, z = partner
        return (tile + y >= 0) & (tile + y < q) & (g + z >= 0) & (g + z < grps)

    def coords(partner):
        h, y, z = partner
        return g + z, ((1 - half) if h else half) * q + tile + y

    barrier = pltpu.get_barrier_semaphore()
    for r in range(1, n):
        pl.semaphore_signal(barrier, inc=1, device_id=(g, (m + r) % n), device_id_type=MESH)
    far = [p for p in PARTNERS if p[2] != 0]
    for p in far:

        @pl.when(has(p))
        def _():
            pl.semaphore_signal(barrier, inc=1, device_id=coords(p), device_id_type=MESH)

    (feat, w1, w2, wm, wo, wc, wp, b1, b2, bm, im_leaf, im_mid, im_coarse) = mats
    (local_sem, wsend, wrecv, psend, precv) = sems
    loads = [
        pltpu.make_async_copy(source, target, local_sem.at[i])
        for i, (source, target) in enumerate(
            [(w1_any, w1), (w2_any, w2), (wm_any, wm), (wo_any, wo), (wc_any, wc.at[m]), (wp_any, wp.at[m]), (feat_any, feat)]
        )
    ]
    for load in loads[-1:] + loads[:-1]:
        load.start()

    def piece_of(level, partner):
        h, y, z = partner
        volume, caps = level["v"], level["caps"]
        length = volume.shape[0]
        pick_x = pl.ds((1 - half) * (length - 1), 1) if h else slice(None)
        pick_y = slice(None) if y == 0 else (pl.ds(length - 1, 1) if y > 0 else pl.ds(0, 1))
        if z == 0:
            return volume.at[pick_x, pick_y]
        return caps.at[1 if z > 0 else 0, pick_x, pick_y]

    def copy_to(level, index):
        h, y, z = PARTNERS[index]
        back = PARTNERS.index((h, -y, -z))
        return pltpu.make_async_remote_copy(
            src_ref=piece_of(level, PARTNERS[index]),
            dst_ref=level["got"][back],
            send_sem=level["send"].at[index],
            recv_sem=level["recv"].at[back],
            device_id=coords(PARTNERS[index]),
            device_id_type=MESH,
        )

    order = sorted(range(len(PARTNERS)), key=lambda i: -sum(abs(s) for s in PARTNERS[i]))

    def caps_of(level):
        volume, caps = level["v"], level["caps"]
        length = volume.shape[0]
        caps[0] = volume[:, :, 0:1, :]
        caps[1] = volume[:, :, length - 1 : length, :]

    def send(level):
        for i in order:

            @pl.when(has(PARTNERS[i]))
            def _():
                copy_to(level, i).start()

    def receive(level):
        for i in order:
            h, y, z = PARTNERS[i]

            @pl.when(has((h, -y, -z)))
            def _():
                copy_to(level, i).wait_recv()

    def extend(level):
        volume, ext, caps = level["v"], level["ext"], level["caps"]
        length, lanes = volume.shape[0], volume.shape[3]
        middle = lanes // 2
        lane = lax.broadcasted_iota(jnp.int32, (1, 1, 1, lanes), 3)
        upper = (lane >= middle).astype(jnp.int32)
        ext[1 : length + 1, 1 : length + 1, 1 : length + 1, :] = volume[...]
        firsts = {}
        for p in [(0, 0, 0)] + PARTNERS:
            a, b = coords(p)
            firsts[p] = jnp.where(has(p), (a * n + b) * 2, -8)

        def source_at(step):
            return slice(0, length) if step == 0 else (slice(0, 1) if step > 0 else slice(length - 1, length))

        def target_at(step):
            return slice(1, length + 1) if step == 0 else (slice(0, 1) if step < 0 else slice(length + 1, length + 2))

        for column, (x, y, z) in enumerate(OFFSETS):
            if (x, y, z) == (0, 0, 0):
                continue
            wanted = jnp.where(upper == 1, neigh[1, column], neigh[0, column])
            shape = tuple(length if s == 0 else 1 for s in (x, y, z)) + (lanes,)
            wanted = jnp.broadcast_to(wanted, shape)
            upper_full = jnp.broadcast_to(upper, shape)
            value = jnp.zeros(shape, F32)
            for h in (0, 1) if x else (0,):
                for cy in (0, y) if y else (0,):
                    for cz in (0, z) if z else (0,):
                        p = (h, cy, cz)
                        at_x = slice(0, 1) if h else source_at(x)
                        at_y = slice(0, 1) if cy else source_at(y)
                        at_z = slice(0, 1) if cz else source_at(z)
                        if p == (0, 0, 0):
                            if z:
                                found = caps[0 if z > 0 else 1, at_x, at_y, :, :]
                            else:
                                found = volume[at_x, at_y, at_z, :]
                        else:
                            found = level["got"][PARTNERS.index(p)][at_x, at_y, at_z, :]
                        swapped = jnp.concatenate([found[..., middle:], found[..., :middle]], axis=3)
                        value = jnp.where(
                            wanted == firsts[p] + upper_full,
                            found,
                            jnp.where(wanted == firsts[p] + 1 - upper_full, swapped, value),
                        )
            ext[target_at(x), target_at(y), target_at(z), :] = value

    taps = wc.shape[1]

    pairs = n // 2
    pair, core = m // 2, m % 2
    partner = pair * 2 + 1 - core

    def weight_copies(part, role, r):
        first, last = taps * part // PIECES, taps * (part + 1) // PIECES
        other = (pair + pairs - r) % pairs * 2
        owner, came = [(m, partner), (m, other + core), (other + core, other + 1 - core)][role]
        target = (pair + r) % pairs * 2 + core if role == 1 else partner
        lane = (0, r, pairs - 1 + r)[role]

        def copy(who):
            spot = wc.at[who, pl.ds(first, last - first)]
            return pltpu.make_async_remote_copy(
                src_ref=spot,
                dst_ref=spot,
                send_sem=wsend.at[part, lane],
                recv_sem=wrecv.at[part, lane],
                device_id=(g, target),
                device_id_type=MESH,
            )

        return functools.partial(copy, owner), functools.partial(copy, came)

    def project_copy(r, other):
        return pltpu.make_async_remote_copy(
            src_ref=wp.at[other],
            dst_ref=wp.at[other],
            send_sem=psend.at[r - 1],
            recv_sem=precv.at[r - 1],
            device_id=(g, (m + r) % n),
            device_id_type=MESH,
        )

    def send_weights(part):
        for r in range(1, pairs):
            weight_copies(part, 1, r)[0]().start()
        weight_copies(part, 0, 0)[0]().start()

    def hand_on(part):
        for r in range(1, pairs):
            weight_copies(part, 1, r)[1]().wait_recv()
            weight_copies(part, 2, r)[0]().start()

    def diagonal(matrix):
        empty = jnp.zeros_like(matrix)
        return jnp.concatenate([matrix, empty], axis=1), jnp.concatenate([empty, matrix], axis=1)

    def fill_diagonal(weights, target):
        rows, width = weights.shape[1], 2 * weights.shape[2]
        for t in range(weights.shape[0]):
            top, bottom = diagonal(weights[t])
            at = (t % 9) * width
            target[t // 9, 0:rows, at : at + width] = top
            target[t // 9, rows : 2 * rows, at : at + width] = bottom

    def fill_upright(weights, target):
        rows, width = weights.shape[1:]
        for t in range(weights.shape[0]):
            empty = jnp.zeros((rows, width), BF16)
            for b in range(slots):
                at = (t % 9 * slots + b) * rows
                for other in range(slots):
                    there = weights[t] if other == b else empty
                    target[t // 9, at : at + rows, other * width : (other + 1) * width] = there

    def convolve_leaf(level, weights):
        ext, length, lanes = level["ext"], edge, level["v"].shape[3]
        for k in range(9):
            y, z = k // 3, k % 3
            rows = ext[:, y : y + length, z : z + length, :].reshape(length + 2, length * length, lanes)
            im_leaf[:, :, k * lanes : (k + 1) * lanes] = rows.astype(BF16)
        total = None
        for x in range(3):
            window = im_leaf[x : x + length].reshape(length**3, 9 * lanes)
            term = matmul_nt(window, weights[x])
            total = term if total is None else total + term
        return rounded_gelu(total)

    leaf_a, leaf_b, mid, low = levels
    loads[-1].wait()
    packed = feat[...].reshape(slots * c0, voxels).astype(F32)
    leaf_a["v"][...] = packed.T.reshape(edge, edge, edge, slots * c0)
    caps_of(leaf_a)
    peers = n - 1
    for p in far:
        peers = peers + has(p).astype(jnp.int32)
    pl.semaphore_wait(barrier, peers)

    send(leaf_a)
    loads[0].wait()
    fill_diagonal(w1, b1)
    loads[4].wait()
    loads[5].wait()
    send_weights(0)
    for r in range(1, n):
        project_copy(r, m).start()
    receive(leaf_a)
    send_weights(1)
    extend(leaf_a)
    first = convolve_leaf(leaf_a, b1)

    leaf_b["v"][...] = first.astype(F32).reshape(edge, edge, edge, slots * c0)
    caps_of(leaf_b)
    send(leaf_b)
    loads[1].wait()
    fill_diagonal(w2, b2)
    hand_on(0)
    receive(leaf_b)
    send_weights(2)
    extend(leaf_b)
    second = convolve_leaf(leaf_b, b2)

    def halving(length):
        small = length // 2
        row = lax.broadcasted_iota(jnp.int32, (small**3, length**3), 0)
        column = lax.broadcasted_iota(jnp.int32, (small**3, length**3), 1)
        x, y, z = column // (length * length), column // length % length, column % length
        hit = row == (x // 2) * small * small + (y // 2) * small + z // 2
        return jnp.where(hit, 0.125, 0.0).astype(BF16)

    side = edge // 2
    pooled = jnp.dot(halving(edge), second, preferred_element_type=F32).astype(BF16).astype(F32)
    for x in range(side):
        for y in range(side):
            at = (x * side + y) * side
            mid["v"][x, y] = pooled[at : at + side]
    caps_of(mid)
    send(mid)
    loads[2].wait()
    fill_upright(wm, bm)
    hand_on(1)
    receive(mid)
    extend(mid)
    lanes = slots * c0
    for k in range(9):
        ty, tz = k // 3, k % 3
        for y in range(side):
            im_mid[:, y * side : (y + 1) * side, k * lanes : (k + 1) * lanes] = mid["ext"][:, y + ty, tz : tz + side, :]
    total = None
    for x in range(3):
        window = im_mid[x : x + side].astype(BF16).reshape(side**3, 9 * lanes)
        term = jnp.dot(window, bm[x], preferred_element_type=F32)
        total = term if total is None else total + term
    middle = rounded_gelu(total)

    small = side // 2
    pooled = jnp.dot(halving(side), middle, preferred_element_type=F32).astype(BF16).astype(F32)
    for x in range(small):
        for y in range(small):
            at = (x * small + y) * small
            low["v"][x, y] = pooled[at : at + small]
    caps_of(low)
    send(low)
    loads[3].wait()
    skip_top, skip_bottom = diagonal(wo[:, :c0])
    lift_top, lift_bottom = diagonal(wo[:, c0:])
    skip_weights = jnp.concatenate([skip_top, skip_bottom], axis=0)
    lift_weights = jnp.concatenate([lift_top, lift_bottom], axis=0)
    mixed = matmul_nt(skip_weights, second)
    hand_on(2)
    for part in range(PIECES):
        weight_copies(part, 0, 0)[1]().wait_recv()
        for r in range(1, pairs):
            weight_copies(part, 2, r)[1]().wait_recv()
    for r in range(1, n):
        project_copy(r, (m + n - r) % n).wait_recv()
    receive(low)
    extend(low)
    cells = small**3
    for t in range(taps):
        tx, ty, tz = t // 9, t // 3 % 3, t % 3
        for b in range(slots):
            for x in range(small):
                for y in range(small):
                    at = b * cells + (x * small + y) * small
                    im_coarse[at : at + small, t * c1 : (t + 1) * c1] = low["ext"][
                        x + tx, y + ty, tz : tz + small, b * c1 : (b + 1) * c1
                    ]
    total = None
    c2 = n * wc.shape[2]
    for t in range(taps):
        term = matmul_nt(im_coarse[:, t * c1 : (t + 1) * c1].astype(BF16), wc[:, t].reshape(c2, c1))
        total = term if total is None else total + term
    hidden = rounded_gelu(total)
    coarse = jnp.dot(hidden, wp[...].reshape(c2, c0), preferred_element_type=F32)
    coarse = jnp.concatenate([coarse[b * cells : (b + 1) * cells] for b in range(slots)], axis=1).astype(BF16)
    row = lax.broadcasted_iota(jnp.int32, (voxels, cells), 0)
    column = lax.broadcasted_iota(jnp.int32, (voxels, cells), 1)
    factor = edge // small
    x, y, z = row // (edge * edge), row // edge % edge, row % edge
    spread = column == (x // factor) * small * small + (y // factor) * small + z // factor
    spread = jnp.where(spread, 1.0, 0.0).astype(BF16)
    widened = jnp.dot(spread, coarse, preferred_element_type=F32).astype(BF16)
    mixed = mixed + matmul_nt(lift_weights, widened)
    owner = lax.broadcasted_iota(jnp.int32, mixed.shape, 0) // c0
    mixed = jnp.where(owner < live[0], mixed, 0.0).astype(BF16)
    for b in range(slots):
        out[b] = mixed[b * c0 : (b + 1) * c0]

    for level in levels:
        for i in order:

            @pl.when(has(PARTNERS[i]))
            def _():
                copy_to(level, i).wait_send()

    for r in range(1, n):
        project_copy(r, m).wait_send()
    for part in range(PIECES):
        weight_copies(part, 0, 0)[0]().wait_send()
        for r in range(1, pairs):
            weight_copies(part, 1, r)[0]().wait_send()
            weight_copies(part, 2, r)[0]().wait_send()


def level_scratch(length, lanes):
    def got(partner):
        h, y, z = partner
        return pltpu.VMEM((1 if h else length, 1 if y else length, 1 if z else length, lanes), F32)

    return dict(
        v=pltpu.VMEM((length, length, length, lanes), F32),
        caps=pltpu.VMEM((2, length, length, 1, lanes), F32),
        ext=pltpu.VMEM((length + 2,) * 3 + (lanes,), F32),
        got=[got(p) for p in PARTNERS],
        send=pltpu.SemaphoreType.DMA((len(PARTNERS),)),
        recv=pltpu.SemaphoreType.DMA((len(PARTNERS),)),
    )


def shards(grps, n, features, live_counts, neighbours, w_first, w_second, w_middle, w_coarse, w_project, w_output):
    slots, c0, voxels = features.shape
    edge = round(voxels ** (1 / 3))
    w_middle = jnp.swapaxes(w_middle, 1, 2)
    taps, _, c1 = w_middle.shape
    lanes = slots * c0
    side, small = edge // 2, edge // 4
    levels = [
        level_scratch(edge, lanes),
        level_scratch(edge, lanes),
        level_scratch(side, lanes),
        level_scratch(small, slots * c1),
    ]
    mats = [
        pltpu.VMEM(features.shape, BF16),
        pltpu.VMEM(w_first.shape, BF16),
        pltpu.VMEM(w_second.shape, BF16),
        pltpu.VMEM(w_middle.shape, BF16),
        pltpu.VMEM(w_output.shape, BF16),
        pltpu.VMEM((n,) + w_coarse.shape, BF16),
        pltpu.VMEM((n,) + w_project.shape, BF16),
        pltpu.VMEM((3, lanes, 9 * lanes), BF16),
        pltpu.VMEM((3, lanes, 9 * lanes), BF16),
        pltpu.VMEM((3, 9 * lanes, slots * c1), BF16),
        pltpu.VMEM((edge + 2, edge * edge, 9 * lanes), BF16),
        pltpu.VMEM((side + 2, side * side, 9 * lanes), F32),
        pltpu.VMEM((slots * small**3, taps * c1), F32),
    ]
    sems = [
        pltpu.SemaphoreType.DMA((7,)),
        pltpu.SemaphoreType.DMA((PIECES, n - 1)),
        pltpu.SemaphoreType.DMA((PIECES, n - 1)),
        pltpu.SemaphoreType.DMA((n - 1,)),
        pltpu.SemaphoreType.DMA((n - 1,)),
    ]
    smem = pl.BlockSpec(memory_space=pltpu.SMEM)
    vmem = pl.BlockSpec(memory_space=pltpu.VMEM)
    stay = pl.BlockSpec(memory_space=pl.ANY)
    return pl.pallas_call(
        functools.partial(kernel, grps, n),
        out_shape=jax.ShapeDtypeStruct(features.shape, BF16),
        in_specs=[stay, smem, smem] + [stay] * 6,
        out_specs=vmem,
        scratch_shapes=[levels, mats, sems],
        compiler_params=pltpu.CompilerParams(collective_id=0, has_side_effects=True),
    )(features, live_counts, neighbours, w_first, w_second, w_middle, w_coarse, w_project, w_output)


def solution(mesh):
    in_specs = (
        P(("grp", "ch"), None, None),
        P(("grp", "ch")),
        P(("grp", "ch"), None),
        P(),
        P(),
        P(),
        P(None, "ch", None),
        P("ch", None),
        P(),
    )
    return jax.shard_map(
        functools.partial(shards, mesh.shape["grp"], mesh.shape["ch"]),
        mesh=mesh,
        in_specs=in_specs,
        out_specs=P(("grp", "ch"), None, None),
        check_vma=False,
    )
```
